32 devices in a mesh: jpair: 2 (over x), blk: 16 (over z, y, core).
Axes of the slice: x: 2, y: 2, z: 4, core: 2. Of those that a mesh axis runs over, the one named last changes fastest.
Arguments:
- dipole: bfloat16 [256, 12, 3, 256, 256], P('blk'), may hold values from -24 to 24
- block_cols: int32 [256, 12], P('blk'), may hold values from 0 to 255, as said below
- upper_vecs: bfloat16 [131072, 256], P(('jpair', 'blk')), parts along dimension 0, may hold values from -0.0234375 to 0.0234375
- lower_vecs: bfloat16 [131072, 128], P(('jpair', 'blk')), parts along dimension 0, may hold values from -0.0234375 to 0.0234375
- upper_energy: float32 [512], P('jpair'), parts along dimension 0, may hold values from 1 to 2
- lower_energy: float32 [256], P('jpair'), parts along dimension 0, may hold values from 0 to 0.8
Outputs:
- strength: float32 [512, 128], P(('jpair', 'blk')), parts along dimension 0
- intensity: float32 [512, 128], P(('jpair', 'blk')), parts along dimension 0
The draws below stay inside these ranges and needn't reach their ends.
There are 2 independent parts, one for each index of `jpair`. The reference program is written for one: setup_inputs(seed, part) draws one part's arguments, and reference() takes and returns one part's arrays. A program takes and returns all parts, laid end to end along the dimension named above; an argument that names none is the same for every part. Nothing has to cross between parts.
Inputs may be any that keep to these rules, and one draw needn't show every extreme that they name: `block_cols`: within one block row the 12 block columns are distinct, and one of them is the row's own index. Splitting the block rows into 16 equal runs of consecutive rows, the columns of one run that fall in another run number at most 12 distinct blocks for each other run, and exactly 12 for some.
All inputs are finite; a program needn't handle non-finite values.
Results may differ from the reference program's by a relative error of at most 0.0026.
Values may be sent and summed in bfloat16 or wider, within the bound.
A program may use at most 256 MiB of HBM per device.

```python
import jax
import jax.numpy as jnp
from jax import lax

NB = 65536
BS = 256
NZ = 12
NU = 256
NL = 128
NBR = 256
N_BLK = 16


def draw_block_cols(key, part):
    per_dev = NBR // N_BLK
    others = N_BLK - 1
    slots = (NZ - 1) * per_dev

    def one_device(device):
        dev_key = jax.random.fold_in(key, device)
        order = jax.random.permutation(jax.random.fold_in(dev_key, 1), others).astype(jnp.int32) + 1
        starts = jax.random.randint(jax.random.fold_in(dev_key, 2), (others,), 0, per_dev).astype(jnp.int32)
        slot_ids = jnp.arange(slots, dtype=jnp.int32)
        which = slot_ids % others
        copy_num = slot_ids // others
        owner = (device + order[which]) % N_BLK
        local_id = (starts[which] + copy_num) % per_dev
        picked = (owner * per_dev + local_id).reshape(NZ - 1, per_dev).T
        own_ids = device * per_dev + jnp.arange(per_dev, dtype=jnp.int32)
        return jnp.concatenate([own_ids[:, None], picked], axis=1)
    device_ids = jnp.arange(N_BLK, dtype=jnp.int32)
    return jax.vmap(one_device)(device_ids).reshape(NBR, NZ).astype(jnp.int32)


def levels(stream_key, extent, split, smallest, high):
    level, own = 1.0, jax.random.fold_in(stream_key, 6)
    for position, shards_of in split:
        draws = jnp.exp(jax.random.uniform(jax.random.fold_in(own, position), (shards_of,), jnp.float32, smallest / len(split), high / len(split)))
        level = level * jnp.repeat(draws, extent[position] // shards_of).reshape([-1 if axis == position else 1 for axis in range(len(extent))])
    return level


def noise(rng, extent, width, most, cuts=(), kind=jnp.bfloat16):
    entries = width * jax.random.normal(rng, extent, jnp.float32)
    if cuts:
        entries = entries * levels(rng, extent, cuts, -0.22, 0.18)
    return jnp.clip(entries, -most, most).astype(kind)


def setup_inputs(seed: int = 0, part: int = 0) -> dict:
    keys = jax.random.split(jax.random.key(seed), 7)
    own_keys = jax.random.split(jax.random.fold_in(keys[6], part), 7)
    dipole = noise(keys[0], (NBR, NZ, 3, BS, BS), 4.0, 24.0, ((0, 16),))
    block_cols = draw_block_cols(jax.random.fold_in(keys[6], 71), part)
    upper_vecs = noise(own_keys[2], (NB, NU), NB ** -0.5, 0.0234375, ((0, 16),))
    lower_vecs = noise(own_keys[3], (NB, NL), NB ** -0.5, 0.0234375, ((0, 16),))
    upper_energy = jnp.clip(jax.random.uniform(own_keys[4], (NU,), jnp.float32, 1.0, 2.0), 1.0, 2.0)
    lower_energy = jnp.clip(jax.random.uniform(own_keys[5], (NL,), jnp.float32, 0.0, 0.8), 0.0, 0.8)
    return {"dipole": dipole, "block_cols": block_cols, "upper_vecs": upper_vecs, "lower_vecs": lower_vecs, "upper_energy": upper_energy, "lower_energy": lower_energy}


THERMAL = 0.3


def reference(dipole, block_cols, upper_vecs, lower_vecs, upper_energy, lower_energy):
    upper_blocks = upper_vecs.reshape(NBR, BS, NU)
    lower_blocks = lower_vecs.reshape(NBR, BS, NL)

    def one_row(running, row_inputs):
        dip_blocks, col_ids, up_rows = row_inputs
        halves = jnp.einsum("kast,su->katu", dip_blocks.astype(jnp.float32), up_rows.astype(jnp.float32)).astype(jnp.bfloat16)
        low_rows = lower_blocks[col_ids.astype(jnp.int32)]
        running = running + jnp.einsum("katu,ktl->aul", halves.astype(jnp.float32), low_rows.astype(jnp.float32))
        return running, None

    start_sum = jnp.zeros((3, NU, NL), jnp.float32)
    proj, _ = lax.scan(one_row, start_sum, (dipole, block_cols, upper_blocks))
    strength = jnp.sum(proj * proj, axis=0)
    wavenumber = upper_energy[:, None] - lower_energy[None, :]
    intensity = wavenumber ** 3 * jnp.exp(-lower_energy / THERMAL)[None, :] * strength
    return strength, intensity
```

```python
import functools

import jax
import jax.numpy as jnp
from jax import lax
from jax.experimental import pallas as pl
from jax.experimental.pallas import tpu as pltpu
from jax.sharding import PartitionSpec as P

THERMAL = 0.3
MESH = pl.DeviceIdType.MESH
LANES = 128
SLOTS = 13


def finish(own_share, energy_rows, lower_energy):
    strength = jnp.sum(own_share * own_share, axis=0)
    wavenumber = energy_rows - lower_energy
    intensity = wavenumber * wavenumber * wavenumber * jnp.exp(-lower_energy / THERMAL) * strength
    return strength, intensity


def plain_device(dipole, block_cols, upper_vecs, lower_vecs, upper_energy, lower_energy):
    rows_blk, nonzero, n_comps, block_size, _ = dipole.shape
    upper_count = upper_vecs.shape[1]
    lower_count = lower_vecs.shape[1]
    upper_blocks = upper_vecs.reshape(rows_blk, block_size, upper_count)
    halves = jnp.einsum(
        "rkast,rsu->rkatu", dipole, upper_blocks, preferred_element_type=jnp.float32
    ).astype(jnp.bfloat16)
    gathered = lax.all_gather(lower_vecs, "blk", axis=0, tiled=True)
    all_blocks = gathered.reshape(gathered.shape[0] // block_size, block_size, lower_count)
    lows = jnp.take(all_blocks, block_cols, axis=0)
    proj = jnp.einsum("rkatu,rktl->aul", halves, lows, preferred_element_type=jnp.float32)
    own_share = lax.psum_scatter(proj, "blk", scatter_dimension=1, tiled=True)
    share_rows = own_share.shape[1]
    first_row = lax.axis_index("blk") * share_rows
    energy_rows = lax.dynamic_slice_in_dim(upper_energy, first_row, share_rows, 0)
    return finish(own_share, energy_rows[:, None], lower_energy[None, :])


def kernel(
    grid, first_blocks,
    cols, upper_e, lower_e, d_hbm, u_hbm, l_hbm,
    strength_ref, intensity_ref,
    g0, g1, dbuf, ubuf, ut, proj, send_buf, core_in, core_sum, y_in, y_sum, z_in,
    recv_sem, send_sem, own_sem, d_sem, u_sem, red_send, red_recv,
):
    n_z, n_y = grid
    gathered = (g0, g1)
    rows, entries, block, _ = d_hbm.shape
    n_comps = proj.shape[0]
    nonzero = entries // n_comps
    me = lax.axis_index("blk")
    core = lax.rem(me, 2)
    y = lax.rem(me // 2, n_y)
    z = me // (2 * n_y)
    other_y = 1 - y

    def device(zz, yy, cc):
        return (zz * n_y + yy) * 2 + cc

    sibling = device(z, y, 1 - core)
    across = device(z, other_y, core)

    def d_copy(i):
        half, row = i // rows, lax.rem(i, rows)
        lanes = pl.ds(pl.multiple_of(half * LANES, LANES), LANES)
        slot = lax.rem(i, SLOTS)
        return pltpu.make_async_copy(d_hbm.at[row, :, :, lanes], dbuf.at[slot], d_sem.at[slot])

    u_copy = pltpu.make_async_copy(u_hbm, ubuf, u_sem)

    barrier = pltpu.get_barrier_semaphore()
    pl.semaphore_signal(barrier, inc=1, device_id={"blk": sibling}, device_id_type=MESH)
    pl.semaphore_signal(barrier, inc=1, device_id={"blk": across}, device_id_type=MESH)
    for off in range(1, n_z):
        pl.semaphore_signal(
            barrier, inc=1, device_id={"blk": device(lax.rem(z + off, n_z), y, core)}, device_id_type=MESH
        )
    own_copies = [
        pltpu.make_async_copy(l_hbm.at[:, h], gathered[h].at[pl.ds(me * rows, rows)], own_sem.at[h])
        for h in range(2)
    ]
    pl.semaphore_wait(barrier, n_z + 1)

    spans = ((0, first_blocks), (first_blocks, rows - first_blocks))
    DOWN, UP, CROSS, CORE = range(4)
    targets = (device(z - 1, y, core), device(z + 1, y, core), across, sibling)
    exists = (z > 0, z < n_z - 1, z >= 0, z >= 0)
    pending = []

    def block_copy(h, src, piece, way, own):
        start, size = spans[piece]
        here = gathered[h].at[pl.ds(src * rows + start, size)]
        return pltpu.make_async_remote_copy(
            src_ref=l_hbm.at[pl.ds(start, size), h] if own else here,
            dst_ref=here,
            send_sem=send_sem.at[h, way, src // 2, piece],
            recv_sem=recv_sem.at[h, src, piece],
            device_id={"blk": targets[way]},
            device_id_type=MESH,
        )

    def send(*where):
        @pl.when(exists[where[3]])
        def _():
            block_copy(*where).start()

    def arrived(h, src, piece):
        block_copy(h, src, piece, CORE, False).wait_recv()

    def pass_on(h, guard, src, piece, ways):
        pending.extend((guard, h, src, piece, way, False) for way in ways)

        @pl.when(guard)
        def _():
            arrived(h, src, piece)
            for way in ways:
                send(h, src, piece, way, False)

    def own_sends(h):
        for way, piece in (
            (CROSS, 1), (DOWN, 0), (UP, 0), (CROSS, 0), (DOWN, 1), (UP, 1), (CORE, 0), (CORE, 1)
        ):
            pending.append((z >= 0, h, me, piece, way, True))
            send(h, me, piece, way, True)

    def events(h):
        steps = [functools.partial(pass_on, h, z >= 0, across, 1, (DOWN, UP, CORE))]
        for off in range(1, n_z):
            low, high = z - off >= 0, z + off < n_z
            steps += [
                functools.partial(pass_on, h, low, device(z - off, y, core), 0, (UP, CROSS, CORE)),
                functools.partial(pass_on, h, high, device(z + off, y, core), 0, (DOWN, CROSS, CORE)),
            ]
            if off == 1:
                steps += [functools.partial(pass_on, h, z >= 0, across, 0, (CORE,))]
            else:
                steps += [
                    functools.partial(pass_on, h, z - off + 1 >= 0, device(z - off + 1, other_y, core), 0, (CORE,)),
                    functools.partial(pass_on, h, z + off - 1 < n_z, device(z + off - 1, other_y, core), 0, (CORE,)),
                ]
            for yy in (y, other_y):
                steps += [
                    functools.partial(pass_on, h, low, device(z - off, yy, core), 1, (UP, CORE)),
                    functools.partial(pass_on, h, high, device(z + off, yy, core), 1, (DOWN, CORE)),
                ]
        off = n_z - 1
        steps += [
            functools.partial(pass_on, h, z - off >= 0, device(z - off, other_y, core), 0, (CORE,)),
            functools.partial(pass_on, h, z + off < n_z, device(z + off, other_y, core), 0, (CORE,)),
        ]
        return steps

    def from_sibling(h):
        own_copies[h].wait()

        def one(i, carry):
            src = i * 2 + 1 - core
            arrived(h, src, 0)
            arrived(h, src, 1)
            return carry

        lax.fori_loop(0, n_z * n_y, one, 0)

    def products(h, lo, hi):
        def one_row(r, carry):
            i = h * rows + r
            d_copy(i).wait()
            slot = lax.rem(i, SLOTS)

            def one_comp(a, inner):
                total = None
                for k in range(0, nonzero, 2):
                    left = jnp.concatenate(
                        [dbuf[slot, k * n_comps + a], dbuf[slot, (k + 1) * n_comps + a]], axis=1
                    )
                    right = jnp.concatenate(
                        [gathered[h][cols[r * nonzero + k]], gathered[h][cols[r * nonzero + k + 1]]], axis=0
                    )
                    term = jnp.dot(left, right, preferred_element_type=jnp.float32)
                    total = term if total is None else total + term
                high = total.astype(jnp.bfloat16)
                low = (total - high.astype(jnp.float32)).astype(jnp.bfloat16)
                both = jnp.dot(
                    ut[r], jnp.concatenate([high, low], axis=1), preferred_element_type=jnp.float32
                )
                proj[a] += both[:, :LANES] + both[:, LANES:]
                return inner

            lax.fori_loop(0, n_comps, one_comp, 0)

            @pl.when(i + SLOTS < 2 * rows)
            def _():
                d_copy(i + SLOTS).start()

            return carry

        lax.fori_loop(lo, hi, one_row, 0)

    own_sends(0)
    u_copy.start()
    own_copies[0].start()
    own_copies[1].start()

    def prefetch(i, carry):
        d_copy(i).start()
        return carry

    lax.fori_loop(0, min(SLOTS, 2 * rows), prefetch, 0)
    proj[...] = jnp.zeros_like(proj)
    u_copy.wait()

    def turn(r, carry):
        ut[r] = ubuf[r].astype(jnp.float32).T.astype(jnp.bfloat16)
        return carry

    lax.fori_loop(0, rows, turn, 0)

    for step in events(0):
        step()
    own_sends(1)
    from_sibling(0)
    steps = events(1)
    chunks = min(8, rows)
    done = 0
    for n, step in enumerate(steps):
        step()
        goal = (n + 1) * chunks // len(steps)
        if goal > done:
            products(0, done * rows // chunks, goal * rows // chunks)
            done = goal
    from_sibling(1)
    products(1, 0, rows)

    n_dev = 2 * n_y * n_z
    share = strength_ref.shape[0]
    for i in range(n_dev):
        send_buf[i // 2, i % 2] = proj[:, i * share:(i + 1) * share, :]

    def reduce_copy(src, dst, slot, target):
        return pltpu.make_async_remote_copy(
            src_ref=src, dst_ref=dst, send_sem=red_send.at[slot], recv_sem=red_recv.at[slot],
            device_id={"blk": target}, device_id_type=MESH,
        )

    copy = reduce_copy(send_buf.at[:, 1 - core], core_in, 0, sibling)
    copy.start()
    copy.wait()
    for i in range(n_z * n_y):
        core_sum[i % n_y, i // n_y] = send_buf[i, core] + core_in[i]
    copy = reduce_copy(core_sum.at[other_y], y_in, 1, across)
    copy.start()
    copy.wait()
    y_sum[...] = core_sum[y] + y_in[...]
    copies = []
    for off in range(1, n_z):
        to = lax.rem(z + off, n_z)
        copy = reduce_copy(y_sum.at[to], z_in.at[off - 1], 1 + off, device(to, y, core))
        copy.start()
        copies.append(copy)
    total = y_sum[z]
    for off, copy in enumerate(copies):
        copy.wait()
        total = total + z_in[off]

    places = lax.broadcasted_iota(jnp.int32, (share, LANES), 0)
    energy_rows = jnp.zeros((share, LANES), jnp.float32)
    for j in range(share):
        energy_rows = jnp.where(places == j, upper_e[me * share + j], energy_rows)
    strength_ref[...], intensity_ref[...] = finish(total, energy_rows, lower_e[...])

    for guard, *where in pending:
        @pl.when(jnp.logical_and(guard, exists[where[3]]))
        def _():
            block_copy(*where).wait_send()


def kernel_device(grid, dipole, block_cols, upper_vecs, lower_vecs, upper_energy, lower_energy):
    rows, nonzero, n_comps, block, _ = dipole.shape
    upper_count = upper_vecs.shape[1]
    lower_count = lower_vecs.shape[1]
    n_z, n_y = grid
    n_dev = 2 * n_y * n_z
    share = upper_count // n_dev
    balance = (n_z * n_y - 2 * n_y + 1) / (2 * (n_z - 1) * (n_y - 1))
    first_blocks = min(rows - 1, max(1, round(rows * balance)))
    f32, bf16 = jnp.float32, jnp.bfloat16
    out = jax.ShapeDtypeStruct((share, lower_count), f32)
    dma = pltpu.SemaphoreType.DMA
    return tuple(pl.pallas_call(
        functools.partial(kernel, grid, first_blocks),
        out_shape=(out, out),
        in_specs=[
            pl.BlockSpec(memory_space=pltpu.SMEM),
            pl.BlockSpec(memory_space=pltpu.SMEM),
            pl.BlockSpec(memory_space=pltpu.VMEM),
            pl.BlockSpec(memory_space=pl.ANY),
            pl.BlockSpec(memory_space=pl.ANY),
            pl.BlockSpec(memory_space=pl.ANY),
        ],
        out_specs=(pl.BlockSpec(memory_space=pltpu.VMEM), pl.BlockSpec(memory_space=pltpu.VMEM)),
        scratch_shapes=[
            pltpu.VMEM((n_dev * rows, block // 2, lower_count), bf16),
            pltpu.VMEM((n_dev * rows, block // 2, lower_count), bf16),
            pltpu.VMEM((SLOTS, nonzero * n_comps, block, block // 2), bf16),
            pltpu.VMEM((rows, block, upper_count), bf16),
            pltpu.VMEM((rows, upper_count, block), bf16),
            pltpu.VMEM((n_comps, upper_count, lower_count), f32),
            pltpu.VMEM((n_z * n_y, 2, n_comps, share, lower_count), f32),
            pltpu.VMEM((n_z * n_y, n_comps, share, lower_count), f32),
            pltpu.VMEM((n_y, n_z, n_comps, share, lower_count), f32),
            pltpu.VMEM((n_z, n_comps, share, lower_count), f32),
            pltpu.VMEM((n_z, n_comps, share, lower_count), f32),
            pltpu.VMEM((n_z - 1, n_comps, share, lower_count), f32),
            dma((2, n_dev, 2)),
            dma((2, 4, n_dev // 2, 2)),
            dma((2,)),
            dma((SLOTS,)),
            dma,
            dma((n_z + 1,)),
            dma((n_z + 1,)),
        ],
        compiler_params=pltpu.CompilerParams(
            collective_id=0, has_side_effects=True, vmem_limit_bytes=60 << 20
        ),
    )(
        block_cols.reshape(-1),
        upper_energy,
        lower_energy.reshape(1, lower_count),
        dipole.reshape(rows, nonzero * n_comps, block, block),
        upper_vecs.reshape(rows, block, upper_count),
        lower_vecs.reshape(rows, 2, block // 2, lower_count),
    ))


def solution(mesh):
    grid = {16: (4, 2)}.get(mesh.shape["blk"])
    per_device = functools.partial(kernel_device, grid) if grid else plain_device
    placed = (
        P("blk", None, None, None, None),
        P("blk", None),
        P(("jpair", "blk"), None),
        P(("jpair", "blk"), None),
        P("jpair"),
        P("jpair"),
    )
    return jax.shard_map(
        per_device,
        mesh=mesh,
        in_specs=placed,
        out_specs=(P(("jpair", "blk"), None), P(("jpair", "blk"), None)),
        check_vma=False,
    )
```

```python
import functools

import jax
import jax.numpy as jnp
from jax import lax
from jax.experimental import pallas as pl
from jax.experimental.pallas import tpu as pltpu
from jax.sharding import PartitionSpec as P

THERMAL = 0.3
MESH = pl.DeviceIdType.MESH
LANES = 128
SLOTS = 36
UNROLL = 4


def finish(own_share, energy_rows, lower_energy):
    strength = jnp.sum(own_share * own_share, axis=0)
    wavenumber = energy_rows - lower_energy
    intensity = wavenumber * wavenumber * wavenumber * jnp.exp(-lower_energy / THERMAL) * strength
    return strength, intensity


def plain_device(dipole, block_cols, upper_vecs, lower_vecs, upper_energy, lower_energy):
    rows_blk, nonzero, n_comps, block_size, _ = dipole.shape
    upper_count = upper_vecs.shape[1]
    lower_count = lower_vecs.shape[1]
    upper_blocks = upper_vecs.reshape(rows_blk, block_size, upper_count)
    halves = jnp.einsum(
        "rkast,rsu->rkatu", dipole, upper_blocks, preferred_element_type=jnp.float32
    ).astype(jnp.bfloat16)
    gathered = lax.all_gather(lower_vecs, "blk", axis=0, tiled=True)
    all_blocks = gathered.reshape(gathered.shape[0] // block_size, block_size, lower_count)
    lows = jnp.take(all_blocks, block_cols, axis=0)
    proj = jnp.einsum("rkatu,rktl->aul", halves, lows, preferred_element_type=jnp.float32)
    own_share = lax.psum_scatter(proj, "blk", scatter_dimension=1, tiled=True)
    share_rows = own_share.shape[1]
    first_row = lax.axis_index("blk") * share_rows
    energy_rows = lax.dynamic_slice_in_dim(upper_energy, first_row, share_rows, 0)
    return finish(own_share, energy_rows[:, None], lower_energy[None, :])


def kernel(
    grid, first_blocks,
    cols, d_hbm, u_hbm, l_hbm,
    own_ref,
    g0, g1, dbuf, ubuf, ut, sums, split, send_buf, core_in, core_sum, y_in, y_sum, z_in,
    recv_sem, send_sem, own_sem, d_sem, u_sem, red_send, red_recv,
):
    n_z, n_y = grid
    gathered = (g0, g1)
    rows, nonzero, n_comps, block, _ = d_hbm.shape
    units = n_comps * rows
    me = lax.axis_index("blk")
    core = lax.rem(me, 2)
    y = lax.rem(me // 2, n_y)
    z = me // (2 * n_y)
    other_y = 1 - y

    def device(zz, yy, cc):
        return (zz * n_y + yy) * 2 + cc

    sibling = device(z, y, 1 - core)
    across = device(z, other_y, core)

    def d_copy(i):
        half, comp, row = i // units, lax.rem(i, units) // rows, lax.rem(i, rows)
        lanes = pl.ds(pl.multiple_of(half * LANES, LANES), LANES)
        slot = lax.rem(i, SLOTS)
        return pltpu.make_async_copy(d_hbm.at[row, :, comp, :, lanes], dbuf.at[slot], d_sem.at[slot])

    u_copy = pltpu.make_async_copy(u_hbm, ubuf, u_sem)

    barrier = pltpu.get_barrier_semaphore()
    pl.semaphore_signal(barrier, inc=1, device_id={"blk": sibling}, device_id_type=MESH)
    pl.semaphore_signal(barrier, inc=1, device_id={"blk": across}, device_id_type=MESH)
    for off in range(1, n_z):
        pl.semaphore_signal(
            barrier, inc=1, device_id={"blk": device(lax.rem(z + off, n_z), y, core)}, device_id_type=MESH
        )
    own_copies = [
        pltpu.make_async_copy(l_hbm.at[:, h], gathered[h].at[pl.ds(me * rows, rows)], own_sem.at[h])
        for h in range(2)
    ]
    pl.semaphore_wait(barrier, n_z + 1)

    spans = ((0, first_blocks), (first_blocks, rows - first_blocks))
    DOWN, UP, CROSS, CORE = range(4)
    targets = (device(z - 1, y, core), device(z + 1, y, core), across, sibling)
    exists = (z > 0, z < n_z - 1, z >= 0, z >= 0)
    pending = []

    def block_copy(h, src, piece, way, own):
        start, size = spans[piece]
        here = gathered[h].at[pl.ds(src * rows + start, size)]
        return pltpu.make_async_remote_copy(
            src_ref=l_hbm.at[pl.ds(start, size), h] if own else here,
            dst_ref=here,
            send_sem=send_sem.at[h, way, src // 2, piece],
            recv_sem=recv_sem.at[h, src, piece],
            device_id={"blk": targets[way]},
            device_id_type=MESH,
        )

    def send(*where):
        @pl.when(exists[where[3]])
        def _():
            block_copy(*where).start()

    def arrived(h, src, piece):
        block_copy(h, src, piece, CORE, False).wait_recv()

    def pass_on(h, guard, src, piece, ways):
        pending.extend((guard, h, src, piece, way, False) for way in ways)

        @pl.when(guard)
        def _():
            arrived(h, src, piece)
            for way in ways:
                send(h, src, piece, way, False)

    def own_sends(h):
        for way, piece in (
            (CROSS, 1), (DOWN, 0), (UP, 0), (CROSS, 0), (DOWN, 1), (UP, 1), (CORE, 0), (CORE, 1)
        ):
            pending.append((z >= 0, h, me, piece, way, True))
            send(h, me, piece, way, True)

    def events(h):
        steps = [functools.partial(pass_on, h, z >= 0, across, 1, (DOWN, UP, CORE))]
        for off in range(1, n_z):
            low, high = z - off >= 0, z + off < n_z
            steps += [
                functools.partial(pass_on, h, low, device(z - off, y, core), 0, (UP, CROSS, CORE)),
                functools.partial(pass_on, h, high, device(z + off, y, core), 0, (DOWN, CROSS, CORE)),
            ]
            if off == 1:
                steps += [functools.partial(pass_on, h, z >= 0, across, 0, (CORE,))]
            else:
                steps += [
                    functools.partial(pass_on, h, z - off + 1 >= 0, device(z - off + 1, other_y, core), 0, (CORE,)),
                    functools.partial(pass_on, h, z + off - 1 < n_z, device(z + off - 1, other_y, core), 0, (CORE,)),
                ]
            for yy in (y, other_y):
                steps += [
                    functools.partial(pass_on, h, low, device(z - off, yy, core), 1, (UP, CORE)),
                    functools.partial(pass_on, h, high, device(z + off, yy, core), 1, (DOWN, CORE)),
                ]
        off = n_z - 1
        steps += [
            functools.partial(pass_on, h, z - off >= 0, device(z - off, other_y, core), 0, (CORE,)),
            functools.partial(pass_on, h, z + off < n_z, device(z + off, other_y, core), 0, (CORE,)),
        ]
        return steps

    def from_sibling(h):
        own_copies[h].wait()

        def one(i, carry):
            src = i * 2 + 1 - core
            arrived(h, src, 0)
            arrived(h, src, 1)
            return carry

        lax.fori_loop(0, n_z * n_y, one, 0)

    def products(h, lo, hi):
        def some_units(n, carry):
            first = lo + n * UNROLL
            for j in range(UNROLL):
                d_copy(h * units + first + j).wait()
            for j in range(UNROLL):
                unit = first + j
                slot = lax.rem(h * units + unit, SLOTS)
                row = lax.rem(unit, rows)
                left = jnp.concatenate([dbuf[slot, k] for k in range(nonzero)], axis=1)
                right = jnp.concatenate([gathered[h][cols[row, k]] for k in range(nonzero)], axis=0)
                total = jnp.dot(left, right, preferred_element_type=jnp.float32)
                if h == 0:
                    sums[unit] = total
                else:
                    total = total + sums[unit]
                    high = total.astype(jnp.bfloat16)
                    low = (total - high.astype(jnp.float32)).astype(jnp.bfloat16)
                    split[row, :, :LANES] = high
                    split[row, :, LANES:] = low
            for j in range(UNROLL):
                later = h * units + first + j + SLOTS

                @pl.when(later < 2 * units)
                def _():
                    d_copy(later).start()

            return carry

        lax.fori_loop(0, (hi - lo) // UNROLL, some_units, 0)

    n_dev = 2 * n_y * n_z
    share = own_ref.shape[1]

    def reduce_copy(a, src, dst, slot, target):
        return pltpu.make_async_remote_copy(
            src_ref=src, dst_ref=dst, send_sem=red_send.at[a, slot], recv_sem=red_recv.at[a, slot],
            device_id={"blk": target}, device_id_type=MESH,
        )

    def over_core(a):
        return reduce_copy(a, send_buf.at[a, :, 1 - core], core_in.at[a], 0, sibling)

    def over_y(a):
        return reduce_copy(a, core_sum.at[a, other_y], y_in.at[a], 1, across)

    def over_z(a, off):
        to = lax.rem(z + off, n_z)
        return reduce_copy(a, y_sum.at[a, to], z_in.at[a, off - 1], 1 + off, device(to, y, core))

    def start_core(a):
        both = jnp.dot(ut[...], split[...].reshape(rows * block, 2 * LANES), preferred_element_type=jnp.float32)
        part = both[:, :LANES] + both[:, LANES:]
        for i in range(n_dev):
            send_buf[a, i // 2, i % 2] = part[i * share:(i + 1) * share]
        over_core(a).start()

    def start_y(a):
        over_core(a).wait()
        for i in range(n_z * n_y):
            core_sum[a, i % n_y, i // n_y] = send_buf[a, i, core] + core_in[a, i]
        over_y(a).start()

    def start_z(a):
        over_y(a).wait()
        y_sum[a] = core_sum[a, y] + y_in[a]
        for off in range(1, n_z):
            over_z(a, off).start()

    def close(a):
        total = y_sum[a, z]
        for off in range(1, n_z):
            over_z(a, off).wait()
            total = total + z_in[a, off - 1]
        own_ref[a] = total

    own_sends(0)
    u_copy.start()
    own_copies[0].start()
    own_copies[1].start()

    def prefetch(i, carry):
        d_copy(i).start()
        return carry

    lax.fori_loop(0, min(SLOTS, 2 * units), prefetch, 0)
    u_copy.wait()

    def turn(r, carry):
        lanes = pl.ds(pl.multiple_of(r * block, block), block)
        ut[:, lanes] = ubuf[r].astype(jnp.float32).T.astype(jnp.bfloat16)
        return carry

    lax.fori_loop(0, rows, turn, 0)

    for step in events(0):
        step()
    own_sends(1)
    from_sibling(0)
    steps = events(1)
    chunks = units // UNROLL
    done = 0
    for n, step in enumerate(steps):
        step()
        goal = (n + 1) * chunks // len(steps)
        if goal > done:
            products(0, done * UNROLL, goal * UNROLL)
            done = goal
    from_sibling(1)
    half = rows // 2
    for a in range(n_comps):
        products(1, a * rows, a * rows + half)
        if a > 0:
            start_y(a - 1)
        products(1, a * rows + half, (a + 1) * rows)
        if a > 0:
            start_z(a - 1)
        start_core(a)
    start_y(n_comps - 1)
    start_z(n_comps - 1)
    for a in range(n_comps):
        close(a)

    for guard, *where in pending:
        @pl.when(jnp.logical_and(guard, exists[where[3]]))
        def _():
            block_copy(*where).wait_send()


def kernel_device(grid, dipole, block_cols, upper_vecs, lower_vecs, upper_energy, lower_energy):
    rows, nonzero, n_comps, block, _ = dipole.shape
    upper_count = upper_vecs.shape[1]
    lower_count = lower_vecs.shape[1]
    n_z, n_y = grid
    n_dev = 2 * n_y * n_z
    share = upper_count // n_dev
    balance = (n_z * n_y - 2 * n_y + 1) / (2 * (n_z - 1) * (n_y - 1))
    first_blocks = min(rows - 1, max(1, round(rows * balance)))
    f32, bf16 = jnp.float32, jnp.bfloat16
    dma = pltpu.SemaphoreType.DMA
    own_share = pl.pallas_call(
        functools.partial(kernel, grid, first_blocks),
        out_shape=jax.ShapeDtypeStruct((n_comps, share, lower_count), f32),
        in_specs=[
            pl.BlockSpec(memory_space=pltpu.SMEM),
            pl.BlockSpec(memory_space=pl.ANY),
            pl.BlockSpec(memory_space=pl.ANY),
            pl.BlockSpec(memory_space=pl.ANY),
        ],
        out_specs=pl.BlockSpec(memory_space=pltpu.VMEM),
        scratch_shapes=[
            pltpu.VMEM((n_dev * rows, block // 2, lower_count), bf16),
            pltpu.VMEM((n_dev * rows, block // 2, lower_count), bf16),
            pltpu.VMEM((SLOTS, nonzero, block, block // 2), bf16),
            pltpu.VMEM((rows, block, upper_count), bf16),
            pltpu.VMEM((upper_count, rows * block), bf16),
            pltpu.VMEM((n_comps * rows, block, lower_count), f32),
            pltpu.VMEM((rows, block, 2 * lower_count), bf16),
            pltpu.VMEM((n_comps, n_z * n_y, 2, share, lower_count), f32),
            pltpu.VMEM((n_comps, n_z * n_y, share, lower_count), f32),
            pltpu.VMEM((n_comps, n_y, n_z, share, lower_count), f32),
            pltpu.VMEM((n_comps, n_z, share, lower_count), f32),
            pltpu.VMEM((n_comps, n_z, share, lower_count), f32),
            pltpu.VMEM((n_comps, n_z - 1, share, lower_count), f32),
            dma((2, n_dev, 2)),
            dma((2, 4, n_dev // 2, 2)),
            dma((2,)),
            dma((SLOTS,)),
            dma,
            dma((n_comps, n_z + 1)),
            dma((n_comps, n_z + 1)),
        ],
        compiler_params=pltpu.CompilerParams(
            collective_id=0, has_side_effects=True, vmem_limit_bytes=62 << 20
        ),
    )(
        block_cols,
        dipole,
        upper_vecs.reshape(rows, block, upper_count),
        lower_vecs.reshape(rows, 2, block // 2, lower_count),
    )
    energy_rows = lax.dynamic_slice_in_dim(upper_energy, lax.axis_index("blk") * share, share, 0)
    return finish(own_share, energy_rows[:, None], lower_energy[None, :])


def solution(mesh):
    grid = {16: (4, 2)}.get(mesh.shape["blk"])
    per_device = functools.partial(kernel_device, grid) if grid else plain_device
    placed = (
        P("blk", None, None, None, None),
        P("blk", None),
        P(("jpair", "blk"), None),
        P(("jpair", "blk"), None),
        P("jpair"),
        P("jpair"),
    )
    return jax.shard_map(
        per_device,
        mesh=mesh,
        in_specs=placed,
        out_specs=(P(("jpair", "blk"), None), P(("jpair", "blk"), None)),
        check_vma=False,
    )
```
